32 devices in a mesh: pole: 4 (over x, core), row: 4 (over z), col: 2 (over y).
Axes of the slice: x: 2, y: 2, z: 4, core: 2. Of those that a mesh axis runs over, the one named last changes fastest.
Arguments:
- inverse: bfloat16 [4, 2, 6144, 6144], P('pole', None, 'col', 'row'), may hold values from -0.078125 to 0.078125
- factor: bfloat16 [4, 2, 6144, 512], P('pole', None, ('row', 'col')), may hold values from -6 to 6
- block_mask: int32 [2, 192], P(None, ('row', 'col')), may hold values from 0 to 1
- pole_real: float32 [4], P('pole'), may hold values from -1 to 1
- pole_imaginary: float32 [4], P('pole'), may hold values from -1 to 1
Outputs:
- density: bfloat16 [2, 4, 768, 512], P('col', 'row', 'pole')
The draws below stay inside these ranges and needn't reach their ends.
All inputs are finite; a program needn't handle non-finite values.
Results may differ from the reference program's by a relative error of at most 0.0012.
Values may be sent and summed in bfloat16 or wider, within the bound.
A program may use at most 64 MiB of HBM per device.

```python
import jax
import jax.numpy as jnp
from jax import lax

NA = 6144
W = 256
S = 2
BLK = 32
SW = 512
POLES = 4
ROWS_CR = 768
N_ROW = 4
N_COL = 2


def with_ends(result, key, low, high):
    longest = result.shape.index(max(result.shape))
    spots = []
    for shift in (0, 1):
        where = [jax.random.randint(jax.random.fold_in(key, axis), (), 0, length) for axis, length in enumerate(result.shape)]
        where[longest] = (where[longest] + shift) % result.shape[longest]
        spots.append(tuple(where))
    return result.at[spots[0]].set(low).at[spots[1]].set(high)


def block_scale(own_key, extent, shards, smallest, largest):
    gain, own = 1.0, jax.random.fold_in(own_key, 6)
    for dim, parts in shards:
        draws = jnp.exp(jax.random.uniform(jax.random.fold_in(own, dim), (parts,), jnp.float32, smallest / len(shards), largest / len(shards)))
        gain = gain * jnp.repeat(draws, extent[dim] // parts).reshape([-1 if axis == dim else 1 for axis in range(len(extent))])
    return gain


def normal_values(rng, extent, deviation, bound, split=(), kind=jnp.bfloat16):
    drawn = deviation * jax.random.normal(rng, extent, jnp.float32)
    if split:
        drawn = drawn * block_scale(rng, extent, split, -0.22, 0.18)
    return jnp.clip(drawn, -bound, bound).astype(kind)


def setup_inputs(seed: int = 0) -> dict:
    seeds = jax.random.split(jax.random.key(seed), 6)
    return {
        "inverse": normal_values(seeds[0], (POLES, 2, NA, NA), NA ** -0.5, 0.078125, ((0, 4), (2, 2), (3, 4))),
        "factor": normal_values(seeds[1], (POLES, 2, NA, SW), 1.0, 6.0, ((0, 4), (2, 8))),
        "block_mask": with_ends(jax.random.randint(seeds[2], (S, NA // BLK), 0, 2), jax.random.fold_in(seeds[2], 1), 0, 1).astype(jnp.int32),
        "pole_real": jnp.clip(jax.random.uniform(seeds[3], (POLES,), jnp.float32, -1.0, 1.0) * block_scale(seeds[3], (POLES,), ((0, 4),), -0.4, 0.0), -1.0, 1.0),
        "pole_imaginary": jnp.clip(jax.random.uniform(seeds[4], (POLES,), jnp.float32, -1.0, 1.0) * block_scale(seeds[4], (POLES,), ((0, 4),), -0.4, 0.0), -1.0, 1.0),
    }


def pole_term(inverse_pair, factor_pair, column_mask, weight_real, weight_imaginary):
    inverse_real = inverse_pair[0]
    inverse_imaginary = inverse_pair[1]
    masked_real = factor_pair[0] * column_mask
    masked_imaginary = factor_pair[1] * column_mask
    product_real = jnp.dot(inverse_real, masked_real, preferred_element_type=jnp.float32) - jnp.dot(inverse_imaginary, masked_imaginary, preferred_element_type=jnp.float32)
    product_imaginary = jnp.dot(inverse_real, masked_imaginary, preferred_element_type=jnp.float32) + jnp.dot(inverse_imaginary, masked_real, preferred_element_type=jnp.float32)
    return weight_real * product_real - weight_imaginary * product_imaginary


def reference(inverse, factor, block_mask, pole_real, pole_imaginary):
    row_mask = jnp.repeat(block_mask.T, BLK, axis=0)
    column_mask = jnp.repeat(row_mask, W, axis=1).astype(jnp.bfloat16)

    def accumulate(position, running):
        return running + pole_term(inverse[position], factor[position], column_mask, pole_real[position], pole_imaginary[position])

    density = lax.fori_loop(0, POLES, accumulate, jnp.zeros((NA, SW), jnp.float32))
    return density.reshape(N_COL, N_ROW, ROWS_CR, SW).astype(jnp.bfloat16)
```

```python
import functools

import jax
import jax.numpy as jnp
from jax import lax
from jax.experimental import pallas as pl
from jax.experimental.pallas import tpu as pltpu
from jax.sharding import PartitionSpec as P

W = 256
BLK = 32
LANES = 128
HALF = LANES // 2
TOP = 32000.0
STEPS = 8.0
MESH = pl.DeviceIdType.MESH


def plain(inverse, factor, block_mask, pole_real, pole_imaginary):
    row_mask = jnp.repeat(block_mask.T, BLK, axis=0)
    column_mask = jnp.repeat(row_mask, W, axis=1).astype(jnp.bfloat16)
    masked = factor[0] * column_mask[None]
    inverse_real = inverse[0, 0]
    inverse_imaginary = inverse[0, 1]
    height = inverse_real.shape[0]
    columns_all = masked.shape[2]
    piece = lax.all_gather(masked, "col", axis=1, tiled=True)
    running_real = jnp.dot(inverse_real, piece[0], preferred_element_type=jnp.float32) - jnp.dot(
        inverse_imaginary, piece[1], preferred_element_type=jnp.float32
    )
    running_imaginary = jnp.dot(
        inverse_real, piece[1], preferred_element_type=jnp.float32
    ) + jnp.dot(inverse_imaginary, piece[0], preferred_element_type=jnp.float32)
    weight_real = pole_real[0]
    weight_imaginary = pole_imaginary[0]
    weighted = weight_real * running_real - weight_imaginary * running_imaginary
    row_count = lax.axis_size("row")
    pole_count = lax.axis_size("pole")
    owned = height // (row_count * pole_count)
    reordered = (
        weighted.reshape(row_count, pole_count, owned, columns_all)
        .transpose(1, 0, 2, 3)
        .reshape(height, columns_all)
    )
    density = lax.psum_scatter(reordered, ("pole", "row"), scatter_dimension=0, tiled=True)
    return density.reshape(1, 1, density.shape[0], columns_all).astype(jnp.bfloat16)


def spread(blocks_mask, depth):
    supers, blocks = blocks_mask.shape
    values = blocks_mask.astype(jnp.float32)
    row = lax.broadcasted_iota(jnp.int32, (depth, blocks), 0)
    block = lax.broadcasted_iota(jnp.int32, (depth, blocks), 1)
    low = block * (depth // blocks)
    inside = jnp.logical_and(row >= low, row < low + depth // blocks)
    columns = []
    for s in range(supers):
        chosen = jnp.where(inside, values[s : s + 1, :], 0.0)
        column = jnp.sum(chosen, axis=1, keepdims=True)
        columns.append(jnp.broadcast_to(column, (depth, LANES)))
    return columns


def low_lanes(rows):
    return lax.broadcasted_iota(jnp.int32, (rows, LANES), 1) < HALF


def swap(value):
    return pltpu.roll(value, HALF, 1)


def split(value):
    high = value.astype(jnp.bfloat16).astype(jnp.float32)
    return high, value - high


def encode(value, ref):
    rows = value.shape[0]
    largest = jnp.max(jnp.abs(value), axis=0, keepdims=True)
    level = jnp.ceil(jnp.log2(jnp.maximum(largest, 1e-30)) * STEPS)
    scaled = value * (TOP * jnp.exp2(level * (-1.0 / STEPS)))
    magic = 12582912.0
    whole = (scaled + magic) - magic
    ref[0:rows, :] = whole.astype(jnp.int32).astype(jnp.int16)
    wide = jnp.broadcast_to(level, (16, LANES))
    ref[rows : rows + 16, :] = wide.astype(jnp.int32).astype(jnp.int16)


def decode(ref):
    rows = ref.shape[0] - 16
    level = ref[rows : rows + 16, :].astype(jnp.int32).astype(jnp.float32)[0:1, :]
    scale = jnp.exp2(level * (1.0 / STEPS)) * (1.0 / TOP)
    return ref[0:rows, :].astype(jnp.int32).astype(jnp.float32) * scale


def kernel(
    rows_n,
    real_hbm,
    imaginary_hbm,
    mask_hbm,
    factor_ref,
    inverse_ref,
    out_ref,
    a_own,
    a_far,
    own_f,
    far_wide,
    pack,
    far_pack,
    real_ref,
    imaginary_ref,
    mask_ref,
    far_mask,
    mask_wide,
    rhs_own,
    rhs_wide,
    rhs_narrow,
    part_wide,
    part_narrow,
    core_wide,
    core_narrow,
    x_out_wide,
    x_out_narrow,
    x_in_wide,
    x_in_narrow,
    z_out_wide,
    z_out_narrow,
    z_in_wide,
    z_in_narrow,
    sum_wide,
    sum_narrow,
    load_sem,
    own_sem,
    small_sem,
    y_send,
    y_recv,
    m_send,
    m_recv,
    c_send,
    c_recv,
    x_send,
    x_recv,
    z_send,
    z_recv,
):
    p = lax.axis_index("pole")
    z = lax.axis_index("row")
    y = lax.axis_index("col")
    core = lax.rem(p, 2)
    x = p // 2
    sibling = {"pole": x * 2 + 1 - core}
    across = {"pole": (1 - x) * 2 + core}
    beside = {"col": 1 - y}
    depth = factor_ref.shape[2]
    wides = far_wide.shape[0]
    chunks = wides + 2
    owned = out_ref.shape[2]
    pair = 2 * owned
    group = 4 * owned
    supers = mask_ref.shape[0]
    per_super = (wides + 1) // supers
    steps = 2 * rows_n
    f32 = jnp.float32
    bf16 = jnp.bfloat16

    barrier = pltpu.get_barrier_semaphore()
    pl.semaphore_signal(barrier, inc=1, device_id=sibling, device_id_type=MESH)
    pl.semaphore_signal(barrier, inc=1, device_id=across, device_id_type=MESH)
    pl.semaphore_signal(barrier, inc=1, device_id=beside, device_id_type=MESH)
    for d in range(1, rows_n):
        pl.semaphore_signal(
            barrier, inc=1, device_id={"row": lax.rem(z + d, rows_n)}, device_id_type=MESH
        )

    def partner(j):
        step = rows_n - 1 - j
        if rows_n & (rows_n - 1):
            return lax.rem(z + rows_n - step, rows_n)
        other = 0
        bit = 1
        while bit < rows_n:
            other = other + bit * lax.rem(z // bit + step // bit, 2)
            bit *= 2
        return other

    def load(far, which, j):
        r = partner(lax.rem(j, rows_n))
        h = jnp.where(j < rows_n, 1 - x, x)
        rows = pl.ds(pl.multiple_of(r * group + h * pair, pair), pair)
        side = (1 - y) if far else y
        columns = pl.ds(pl.multiple_of(side * depth, depth), depth)
        target = a_far if far else a_own
        return pltpu.make_async_copy(
            inverse_ref.at[0, which, rows, columns],
            target.at[pl.ds(pl.multiple_of(j * pair, pair), pair), which * depth : (which + 1) * depth],
            load_sem.at[far, which, j],
        )

    own_copy = pltpu.make_async_copy(factor_ref.at[0], own_f, own_sem)

    def gather(n):
        if n < wides:
            source, target = factor_ref.at[0, :, :, pl.ds(n * LANES, LANES)], far_wide.at[n]
        else:
            source, target = pack.at[n - wides], far_pack.at[n - wides]
        return pltpu.make_async_remote_copy(
            src_ref=source,
            dst_ref=target,
            send_sem=y_send.at[n],
            recv_sem=y_recv.at[n],
            device_id=beside,
            device_id_type=MESH,
        )

    masks = pltpu.make_async_remote_copy(
        src_ref=mask_hbm,
        dst_ref=far_mask,
        send_sem=m_send,
        recv_sem=m_recv,
        device_id=beside,
        device_id_type=MESH,
    )

    def pick(n, wide, narrow):
        return wide.at[n] if n < wides else narrow.at[n - wides]

    def core_copy(n, j):
        return pltpu.make_async_remote_copy(
            src_ref=pick(n, part_wide, part_narrow).at[j, 1 - core],
            dst_ref=pick(n, core_wide, core_narrow).at[j],
            send_sem=c_send.at[n, j],
            recv_sem=c_recv.at[n, j],
            device_id=sibling,
            device_id_type=MESH,
        )

    def x_copy(n, j):
        return pltpu.make_async_remote_copy(
            src_ref=pick(n, x_out_wide, x_out_narrow).at[j],
            dst_ref=pick(n, x_in_wide, x_in_narrow).at[j],
            send_sem=x_send.at[n, j],
            recv_sem=x_recv.at[n, j],
            device_id=across,
            device_id_type=MESH,
        )

    def z_copy(n, d):
        return pltpu.make_async_remote_copy(
            src_ref=pick(n, z_out_wide, z_out_narrow).at[d],
            dst_ref=pick(n, z_in_wide, z_in_narrow).at[d],
            send_sem=z_send.at[n, d],
            recv_sem=z_recv.at[n, d],
            device_id={"row": partner(d)},
            device_id_type=MESH,
        )

    small = [
        pltpu.make_async_copy(source, target, small_sem.at[i])
        for i, (source, target) in enumerate(
            ((mask_hbm, mask_ref), (real_hbm, real_ref), (imaginary_hbm, imaginary_ref))
        )
    ]
    for copy in small:
        copy.start()
    own_copy.start()

    def load_all(far):
        def body(j, carry):
            load(far, 0, j).start()
            load(far, 1, j).start()
            return carry

        lax.fori_loop(0, steps, body, 0)

    load_all(0)
    pl.semaphore_wait(barrier, 3 + rows_n - 1)
    for n in range(wides):
        gather(n).start()
        if n == 0:
            masks.start()
    load_all(1)

    own_copy.wait()
    last = slice(wides * LANES, (wides + 1) * LANES)
    low = low_lanes(depth)
    real_last = own_f[0, :, last].astype(f32)
    imaginary_last = own_f[1, :, last].astype(f32)
    pack[0] = jnp.where(low, real_last, swap(imaginary_last)).astype(bf16)
    pack[1] = jnp.where(low, swap(real_last), imaginary_last).astype(bf16)
    gather(wides).start()
    gather(wides + 1).start()

    for copy in small:
        copy.wait()
    weight_real = real_ref[0]
    weight_imaginary = imaginary_ref[0]
    for s, column in enumerate(spread(mask_ref[...], depth)):
        mask_wide[0, s] = column

    def weigh(real, imaginary, mask):
        first = (weight_real * real - weight_imaginary * imaginary) * mask
        second = (weight_real * imaginary + weight_imaginary * real) * (-mask)
        return first, second

    for n in range(wides + 1):
        columns = slice(n * LANES, (n + 1) * LANES)
        sides = weigh(
            own_f[0, :, columns].astype(f32), own_f[1, :, columns].astype(f32), mask_wide[0, n // per_super]
        )
        for i, side in enumerate(sides):
            high, rest = split(side)
            if n == wides:
                high, rest = jnp.where(low, high, swap(rest)), jnp.where(low, swap(high), rest)
            rows = slice(i * depth, (i + 1) * depth)
            rhs_own[rows, 2 * n * LANES : (2 * n + 1) * LANES] = high.astype(bf16)
            rhs_own[rows, (2 * n + 1) * LANES : (2 * n + 2) * LANES] = rest.astype(bf16)

    def fold_wide(value):
        return (value[:, :LANES] + value[:, LANES:]).reshape(2, owned, LANES)

    def fold_narrow(value):
        both = value + swap(value)
        both = both.reshape(4, owned // 2, LANES)
        keep = low_lanes(owned // 2)
        return [jnp.where(keep, both[2 * c], both[2 * c + 1]) for c in range(2)]

    def block(j):
        return pl.ds(pl.multiple_of(j * pair, pair), pair)

    def own_body(j, carry):
        load(0, 0, j).wait()
        load(0, 1, j).wait()
        value = jnp.dot(a_own[block(j), :], rhs_own[...], preferred_element_type=f32)
        for n in range(wides):
            part_wide[n, j] = fold_wide(value[:, 2 * n * LANES : (2 * n + 2) * LANES])
        for k in range(2):
            low_column = (2 * wides + k) * LANES
            folded = fold_narrow(value[:, low_column : low_column + LANES])
            for c in range(2):
                part_narrow[k, j, c] = folded[c]
        return carry

    lax.fori_loop(0, steps, own_body, 0)
    masks.wait_recv()
    for s, column in enumerate(spread(far_mask[...], depth)):
        mask_wide[1, s] = column

    def send_x(n, j):
        core_copy(n, j).wait_recv()
        total = pick(n, part_wide, part_narrow)[j, core] + pick(n, core_wide, core_narrow)[j]
        encode(total, pick(n, x_out_wide, x_out_narrow).at[j])
        x_copy(n, j).start()

    def send_z(n, d):
        j = d + rows_n
        core_copy(n, j).wait_recv()
        x_copy(n, d).wait_recv()
        total = pick(n, part_wide, part_narrow)[j, core] + pick(n, core_wide, core_narrow)[j]
        total = total + decode(pick(n, x_in_wide, x_in_narrow).at[d])

        @pl.when(d < rows_n - 1)
        def _():
            encode(total, pick(n, z_out_wide, z_out_narrow).at[d])
            z_copy(n, d).start()

        @pl.when(d == rows_n - 1)
        def _():
            pick(n, sum_wide, sum_narrow)[...] = total

    def finish(n):
        total = pick(n, sum_wide, sum_narrow)[...]
        for d in range(rows_n - 1):
            z_copy(n, d).wait_recv()
            total = total + decode(pick(n, z_in_wide, z_in_narrow).at[d])
        if n < wides:
            out_ref[0, 0, :, n * LANES : (n + 1) * LANES] = total.astype(bf16)
        return total

    lag = 2

    def compute(n):
        def body(j, carry):
            if n == 0:
                load(1, 0, j).wait()
                load(1, 1, j).wait()
            left = a_far[block(j), :]
            if n < wides:
                value = jnp.dot(left, rhs_wide[...], preferred_element_type=f32)
                part_wide[n, j] += fold_wide(value)
            else:
                value = jnp.dot(left, rhs_narrow[...], preferred_element_type=f32)
                folded = fold_narrow(value)
                for c in range(2):
                    part_narrow[n - wides, j, c] += folded[c]
            core_copy(n, j).start()

            @pl.when(jnp.logical_and(j >= lag, j < rows_n + lag))
            def _():
                send_x(n, j - lag)

            if n >= 1:

                @pl.when(j >= rows_n)
                def _():
                    send_z(n - 1, j - rows_n)

            return carry

        lax.fori_loop(0, steps, body, 0)

    for n in range(chunks):
        gather(n).wait_recv()
        if n < wides:
            sides = weigh(
                far_wide[n, 0].astype(f32), far_wide[n, 1].astype(f32), mask_wide[1, n // per_super]
            )
        else:
            packed = far_pack[n - wides].astype(f32)
            turned = swap(packed)
            sides = weigh(
                jnp.where(low, packed, turned), jnp.where(low, turned, packed), mask_wide[1, supers - 1]
            )
        for i, side in enumerate(sides):
            high, rest = split(side)
            rows = slice(i * depth, (i + 1) * depth)
            if n < wides:
                rhs_wide[rows, :LANES] = high.astype(bf16)
                rhs_wide[rows, LANES:] = rest.astype(bf16)
            else:
                rhs_narrow[rows, :] = jnp.where(low, high, rest).astype(bf16)
        compute(n)
        if 2 <= n < wides + 2:
            if n - 2 < wides:
                finish(n - 2)

    def last_z(d, carry):
        send_z(chunks - 1, d)
        return carry

    lax.fori_loop(0, rows_n, last_z, 0)
    for n in range(max(chunks - 2, 0), wides):
        finish(n)
    first = finish(wides)
    second = finish(wides + 1)
    keep = low_lanes(owned // 2)
    out_ref[0, 0, : owned // 2, last] = jnp.where(keep, first, swap(second)).astype(bf16)
    out_ref[0, 0, owned // 2 :, last] = jnp.where(keep, swap(first), second).astype(bf16)

    masks.wait_send()
    for n in range(chunks):
        gather(n).wait_send()

        def drain(j, carry):
            core_copy(n, j).wait_send()

            @pl.when(j < rows_n)
            def _():
                x_copy(n, j).wait_send()

            @pl.when(j < rows_n - 1)
            def _():
                z_copy(n, j).wait_send()

            return carry

        lax.fori_loop(0, steps, drain, 0)


def fused(inverse, factor, block_mask, pole_real, pole_imaginary):
    rows_n = lax.axis_size("row")
    height, width = inverse.shape[2:]
    depth, columns_all = factor.shape[2:]
    wides = columns_all // LANES - 1
    chunks = wides + 2
    owned = height // (rows_n * 4)
    half = owned // 2
    steps = 2 * rows_n
    f32, bf16, i16 = jnp.float32, jnp.bfloat16, jnp.int16
    dma = pltpu.SemaphoreType.DMA
    big = pl.BlockSpec(memory_space=pltpu.HBM)

    def both(lead, rows, kind):
        return [
            pltpu.VMEM((wides,) + lead + (rows[0], LANES), kind),
            pltpu.VMEM((2,) + lead + (rows[1], LANES), kind),
        ]

    full = (owned, half)
    coded = (owned + 16, half + 16)
    return pl.pallas_call(
        functools.partial(kernel, rows_n),
        out_shape=jax.ShapeDtypeStruct((1, 1, owned, columns_all), jnp.bfloat16),
        in_specs=[big] * 5,
        out_specs=pl.BlockSpec(memory_space=pltpu.VMEM),
        scratch_shapes=[
            pltpu.VMEM((height, 2 * depth), bf16),
            pltpu.VMEM((height, 2 * depth), bf16),
            pltpu.VMEM((2, depth, columns_all), bf16),
            pltpu.VMEM((wides, 2, depth, LANES), bf16),
            pltpu.VMEM((2, depth, LANES), bf16),
            pltpu.VMEM((2, depth, LANES), bf16),
            pltpu.SMEM(pole_real.shape, f32),
            pltpu.SMEM(pole_imaginary.shape, f32),
            pltpu.VMEM(block_mask.shape, block_mask.dtype),
            pltpu.VMEM(block_mask.shape, block_mask.dtype),
            pltpu.VMEM((2, block_mask.shape[0], depth, LANES), f32),
            pltpu.VMEM((2 * depth, 2 * columns_all), bf16),
            pltpu.VMEM((2 * depth, 2 * LANES), bf16),
            pltpu.VMEM((2 * depth, LANES), bf16),
            *both((steps, 2), full, f32),
            *both((steps,), full, f32),
            *both((rows_n,), coded, i16),
            *both((rows_n,), coded, i16),
            *both((rows_n - 1,), coded, i16),
            *both((rows_n - 1,), coded, i16),
            *both((), full, f32),
            dma((2, 2, steps)),
            dma,
            dma((3,)),
            dma((chunks,)),
            dma((chunks,)),
            dma,
            dma,
            dma((chunks, steps)),
            dma((chunks, steps)),
            dma((chunks, rows_n)),
            dma((chunks, rows_n)),
            dma((chunks, rows_n)),
            dma((chunks, rows_n)),
        ],
        compiler_params=pltpu.CompilerParams(
            collective_id=0, has_side_effects=True, vmem_limit_bytes=60 * 1024 * 1024
        ),
    )(pole_real, pole_imaginary, block_mask, factor, inverse)


def solution(mesh):
    sizes = dict(mesh.shape)

    def shards(inverse, factor, block_mask, pole_real, pole_imaginary):
        supers = block_mask.shape[0]
        wide = factor.shape[3] // supers
        small = 2 * inverse.shape[2] * inverse.shape[3] * 2 <= 20 * 1024 * 1024
        fits = sizes["pole"] == 4 and sizes["col"] == 2 and sizes["row"] >= 2
        owned = inverse.shape[2] // (sizes["row"] * 4)
        if fits and small and wide % LANES == 0 and owned % 32 == 0:
            body = fused
        else:
            body = plain
        return body(inverse, factor, block_mask, pole_real, pole_imaginary)

    return jax.shard_map(
        shards,
        mesh=mesh,
        in_specs=(
            P("pole", None, "col", "row"),
            P("pole", None, ("row", "col"), None),
            P(None, ("row", "col")),
            P("pole"),
            P("pole"),
        ),
        out_specs=P("col", "row", "pole", None),
        check_vma=False,
    )
```

```python
import functools

import jax
import jax.numpy as jnp
from jax import lax
from jax.experimental import pallas as pl
from jax.experimental.pallas import tpu as pltpu
from jax.sharding import PartitionSpec as P

W = 256
BLK = 32
LANES = 128
HALF = LANES // 2
TOP = 32000.0
STEPS = 8.0
MESH = pl.DeviceIdType.MESH


def plain(inverse, factor, block_mask, pole_real, pole_imaginary):
    row_mask = jnp.repeat(block_mask.T, BLK, axis=0)
    column_mask = jnp.repeat(row_mask, W, axis=1).astype(jnp.bfloat16)
    masked = factor[0] * column_mask[None]
    inverse_real = inverse[0, 0]
    inverse_imaginary = inverse[0, 1]
    height = inverse_real.shape[0]
    columns_all = masked.shape[2]
    piece = lax.all_gather(masked, "col", axis=1, tiled=True)
    running_real = jnp.dot(inverse_real, piece[0], preferred_element_type=jnp.float32) - jnp.dot(
        inverse_imaginary, piece[1], preferred_element_type=jnp.float32
    )
    running_imaginary = jnp.dot(
        inverse_real, piece[1], preferred_element_type=jnp.float32
    ) + jnp.dot(inverse_imaginary, piece[0], preferred_element_type=jnp.float32)
    weight_real = pole_real[0]
    weight_imaginary = pole_imaginary[0]
    weighted = weight_real * running_real - weight_imaginary * running_imaginary
    row_count = lax.axis_size("row")
    pole_count = lax.axis_size("pole")
    owned = height // (row_count * pole_count)
    reordered = (
        weighted.reshape(row_count, pole_count, owned, columns_all)
        .transpose(1, 0, 2, 3)
        .reshape(height, columns_all)
    )
    density = lax.psum_scatter(reordered, ("pole", "row"), scatter_dimension=0, tiled=True)
    return density.reshape(1, 1, density.shape[0], columns_all).astype(jnp.bfloat16)


def spread(blocks_mask, depth):
    supers, blocks = blocks_mask.shape
    values = blocks_mask.astype(jnp.float32)
    row = lax.broadcasted_iota(jnp.int32, (depth, blocks), 0)
    block = lax.broadcasted_iota(jnp.int32, (depth, blocks), 1)
    low = block * (depth // blocks)
    inside = jnp.logical_and(row >= low, row < low + depth // blocks)
    columns = []
    for s in range(supers):
        chosen = jnp.where(inside, values[s : s + 1, :], 0.0)
        column = jnp.sum(chosen, axis=1, keepdims=True)
        columns.append(jnp.broadcast_to(column, (depth, LANES)))
    return columns


def low_lanes(rows):
    return lax.broadcasted_iota(jnp.int32, (rows, LANES), 1) < HALF


def swap(value):
    return pltpu.roll(value, HALF, 1)


def split(value):
    high = value.astype(jnp.bfloat16).astype(jnp.float32)
    return high, value - high


def encode(value, ref):
    rows = value.shape[0]
    largest = jnp.max(jnp.abs(value), axis=0, keepdims=True)
    level = jnp.ceil(jnp.log2(jnp.maximum(largest, 1e-30)) * STEPS)
    scaled = value * (TOP * jnp.exp2(level * (-1.0 / STEPS)))
    magic = 12582912.0
    whole = (scaled + magic) - magic
    ref[0:rows, :] = whole.astype(jnp.int32).astype(jnp.int16)
    wide = jnp.broadcast_to(level, (16, LANES))
    ref[rows : rows + 16, :] = wide.astype(jnp.int32).astype(jnp.int16)


def decode(ref):
    rows = ref.shape[0] - 16
    level = ref[rows : rows + 16, :].astype(jnp.int32).astype(jnp.float32)[0:1, :]
    scale = jnp.exp2(level * (1.0 / STEPS)) * (1.0 / TOP)
    return ref[0:rows, :].astype(jnp.int32).astype(jnp.float32) * scale


def kernel(
    rows_n,
    real_hbm,
    imaginary_hbm,
    mask_hbm,
    factor_ref,
    inverse_ref,
    out_ref,
    a_own,
    a_far,
    own_f,
    far_wide,
    pack,
    far_pack,
    real_ref,
    imaginary_ref,
    mask_ref,
    far_mask,
    mask_wide,
    rhs_own,
    rhs_wide,
    rhs_narrow,
    part_wide,
    part_narrow,
    core_wide,
    core_narrow,
    x_out_wide,
    x_out_narrow,
    x_in_wide,
    x_in_narrow,
    z_out_wide,
    z_out_narrow,
    z_in_wide,
    z_in_narrow,
    sum_wide,
    sum_narrow,
    load_sem,
    own_sem,
    small_sem,
    y_send,
    y_recv,
    m_send,
    m_recv,
    c_send,
    c_recv,
    x_send,
    x_recv,
    z_send,
    z_recv,
):
    p = lax.axis_index("pole")
    z = lax.axis_index("row")
    y = lax.axis_index("col")
    core = lax.rem(p, 2)
    x = p // 2
    sibling = {"pole": x * 2 + 1 - core}
    across = {"pole": (1 - x) * 2 + core}
    beside = {"col": 1 - y}
    depth = factor_ref.shape[2]
    wides = far_wide.shape[0]
    chunks = wides + 2
    owned = out_ref.shape[2]
    pair = 2 * owned
    group = 4 * owned
    supers = mask_ref.shape[0]
    per_super = (wides + 1) // supers
    steps = 2 * rows_n
    f32 = jnp.float32
    bf16 = jnp.bfloat16

    order = list(range(chunks))

    barrier = pltpu.get_barrier_semaphore()
    pl.semaphore_signal(barrier, inc=1, device_id=sibling, device_id_type=MESH)
    pl.semaphore_signal(barrier, inc=1, device_id=across, device_id_type=MESH)
    pl.semaphore_signal(barrier, inc=1, device_id=beside, device_id_type=MESH)
    for d in range(1, rows_n):
        pl.semaphore_signal(
            barrier, inc=1, device_id={"row": lax.rem(z + d, rows_n)}, device_id_type=MESH
        )

    def partner(j):
        step = rows_n - 1 - j
        if rows_n & (rows_n - 1):
            return lax.rem(z + rows_n - step, rows_n)
        other = 0
        bit = 1
        while bit < rows_n:
            other = other + bit * lax.rem(z // bit + step // bit, 2)
            bit *= 2
        return other

    def load(far, which, j):
        r = partner(lax.rem(j, rows_n))
        h = jnp.where(j < rows_n, 1 - x, x)
        rows = pl.ds(pl.multiple_of(r * group + h * pair, pair), pair)
        side = (1 - y) if far else y
        columns = pl.ds(pl.multiple_of(side * depth, depth), depth)
        target = a_far if far else a_own
        return pltpu.make_async_copy(
            inverse_ref.at[0, which, rows, columns],
            target.at[pl.ds(pl.multiple_of(j * pair, pair), pair), which * depth : (which + 1) * depth],
            load_sem.at[far, which, j],
        )

    def own_copy(n):
        columns = pl.ds(n * LANES, LANES)
        return pltpu.make_async_copy(
            factor_ref.at[0, :, :, columns], own_f.at[:, :, columns], own_sem.at[n]
        )

    def gather(n):
        if n < wides:
            source, target = own_f.at[:, :, pl.ds(n * LANES, LANES)], far_wide.at[n]
        else:
            source, target = pack.at[n - wides], far_pack.at[n - wides]
        return pltpu.make_async_remote_copy(
            src_ref=source,
            dst_ref=target,
            send_sem=y_send.at[n],
            recv_sem=y_recv.at[n],
            device_id=beside,
            device_id_type=MESH,
        )

    masks = pltpu.make_async_remote_copy(
        src_ref=mask_hbm,
        dst_ref=far_mask,
        send_sem=m_send,
        recv_sem=m_recv,
        device_id=beside,
        device_id_type=MESH,
    )

    def pick(n, wide, narrow):
        return wide.at[n] if n < wides else narrow.at[n - wides]

    def core_copy(n, j):
        return pltpu.make_async_remote_copy(
            src_ref=pick(n, part_wide, part_narrow).at[j, 1 - core],
            dst_ref=pick(n, core_wide, core_narrow).at[j],
            send_sem=c_send.at[n],
            recv_sem=c_recv.at[n, j],
            device_id=sibling,
            device_id_type=MESH,
        )

    def x_copy(n, j):
        return pltpu.make_async_remote_copy(
            src_ref=pick(n, x_out_wide, x_out_narrow).at[j],
            dst_ref=pick(n, x_in_wide, x_in_narrow).at[j],
            send_sem=x_send.at[n],
            recv_sem=x_recv.at[n, j],
            device_id=across,
            device_id_type=MESH,
        )

    def z_copy(n, d):
        return pltpu.make_async_remote_copy(
            src_ref=pick(n, z_out_wide, z_out_narrow).at[d],
            dst_ref=pick(n, z_in_wide, z_in_narrow).at[d],
            send_sem=z_send.at[n],
            recv_sem=z_recv.at[n, d],
            device_id={"row": partner(d)},
            device_id_type=MESH,
        )

    small = [
        pltpu.make_async_copy(source, target, small_sem.at[i])
        for i, (source, target) in enumerate(
            ((mask_hbm, mask_ref), (real_hbm, real_ref), (imaginary_hbm, imaginary_ref))
        )
    ]
    for n in range(wides + 1):
        own_copy(n).start()

    def load_all(far):
        def body(j, carry):
            load(far, 0, j).start()
            load(far, 1, j).start()
            return carry

        lax.fori_loop(0, steps, body, 0)

    pl.semaphore_wait(barrier, 3 + rows_n - 1)
    own_copy(0).wait()
    gather(0).start()
    masks.start()
    for copy in small:
        copy.start()
    load_all(0)
    for n in range(1, wides + 1):
        own_copy(n).wait()

    last = slice(wides * LANES, (wides + 1) * LANES)
    low = low_lanes(depth)
    real_last = own_f[0, :, last].astype(f32)
    imaginary_last = own_f[1, :, last].astype(f32)
    pack[0] = jnp.where(low, real_last, swap(imaginary_last)).astype(bf16)
    pack[1] = jnp.where(low, swap(real_last), imaginary_last).astype(bf16)
    for n in order[1:]:
        gather(n).start()
    load_all(1)

    for copy in small:
        copy.wait()
    weight_real = real_ref[0]
    weight_imaginary = imaginary_ref[0]
    for s, column in enumerate(spread(mask_ref[...], depth)):
        mask_wide[0, s] = column

    def weigh(real, imaginary, mask):
        first = (weight_real * real - weight_imaginary * imaginary) * mask
        second = (weight_real * imaginary + weight_imaginary * real) * (-mask)
        return first, second

    for n in range(wides + 1):
        columns = slice(n * LANES, (n + 1) * LANES)
        sides = weigh(
            own_f[0, :, columns].astype(f32), own_f[1, :, columns].astype(f32), mask_wide[0, n // per_super]
        )
        for i, side in enumerate(sides):
            high, rest = split(side)
            if n == wides:
                high, rest = jnp.where(low, high, swap(rest)), jnp.where(low, swap(high), rest)
            rows = slice(i * depth, (i + 1) * depth)
            rhs_own[rows, 2 * n * LANES : (2 * n + 1) * LANES] = high.astype(bf16)
            rhs_own[rows, (2 * n + 1) * LANES : (2 * n + 2) * LANES] = rest.astype(bf16)

    def fold_wide(value):
        return (value[:, :LANES] + value[:, LANES:]).reshape(2, owned, LANES)

    def fold_narrow(value):
        both = value + swap(value)
        both = both.reshape(4, owned // 2, LANES)
        keep = low_lanes(owned // 2)
        return [jnp.where(keep, both[2 * c], both[2 * c + 1]) for c in range(2)]

    def block(j):
        return pl.ds(pl.multiple_of(j * pair, pair), pair)

    def own_body(j, carry):
        load(0, 0, j).wait()
        load(0, 1, j).wait()
        value = jnp.dot(a_own[block(j), :], rhs_own[...], preferred_element_type=f32)
        for n in range(wides):
            part_wide[n, j] = fold_wide(value[:, 2 * n * LANES : (2 * n + 2) * LANES])
        for k in range(2):
            low_column = (2 * wides + k) * LANES
            folded = fold_narrow(value[:, low_column : low_column + LANES])
            for c in range(2):
                part_narrow[k, j, c] = folded[c]
        return carry

    lax.fori_loop(0, steps, own_body, 0)
    masks.wait_recv()
    for s, column in enumerate(spread(far_mask[...], depth)):
        mask_wide[1, s] = column

    def send_x(n, j):
        core_copy(n, j).wait_recv()
        total = pick(n, part_wide, part_narrow)[j, core] + pick(n, core_wide, core_narrow)[j]
        encode(total, pick(n, x_out_wide, x_out_narrow).at[j])
        x_copy(n, j).start()

    def finish(n):
        total = pick(n, sum_wide, sum_narrow)[...]
        for d in range(rows_n - 1):
            z_copy(n, d).wait_recv()
        for d in range(rows_n - 1):
            total = total + decode(pick(n, z_in_wide, z_in_narrow).at[d])
        if n < wides:
            out_ref[0, 0, :, n * LANES : (n + 1) * LANES] = total.astype(bf16)
        else:
            sum_narrow[n - wides] = total
        return total

    def products(n, first, count, per, after=None):
        def body(i, carry):
            begin = first + i * per
            right = rhs_wide[...] if n < wides else rhs_narrow[...]
            for k in range(per):
                j = begin + k
                if n == 0:
                    load(1, 0, j).wait()
                    load(1, 1, j).wait()
            for k in range(per):
                j = begin + k
                value = jnp.dot(a_far[block(j), :], right, preferred_element_type=f32)
                if n < wides:
                    part_wide[n, j] += fold_wide(value)
                else:
                    folded = fold_narrow(value)
                    for c in range(2):
                        part_narrow[n - wides, j, c] += folded[c]
            for k in range(per):
                core_copy(n, begin + k).start()
            if after is not None:
                after(i)
            return carry

        lax.fori_loop(0, count // per, body, 0)

    def send_x_range(n, first, count):
        for j in range(first, first + count):
            core_copy(n, j).wait_recv()
        for j in range(first, first + count):
            total = pick(n, part_wide, part_narrow)[j, core] + pick(n, core_wide, core_narrow)[j]
            encode(total, pick(n, x_out_wide, x_out_narrow).at[j])
        for j in range(first, first + count):
            x_copy(n, j).start()

    def send_z_range(n, first, count):
        chosen = range(first, first + count)
        for d in chosen:
            core_copy(n, d + rows_n).wait_recv()
            x_copy(n, d).wait_recv()
        for d in chosen:
            j = d + rows_n
            total = pick(n, part_wide, part_narrow)[j, core] + pick(n, core_wide, core_narrow)[j]
            total = total + decode(pick(n, x_in_wide, x_in_narrow).at[d])
            if d < rows_n - 1:
                encode(total, pick(n, z_out_wide, z_out_narrow).at[d])
            else:
                pick(n, sum_wide, sum_narrow)[...] = total
        for d in chosen:
            if d < rows_n - 1:
                z_copy(n, d).start()

    def sent(source, sem, target):
        pltpu.make_async_remote_copy(
            src_ref=source,
            dst_ref=source,
            send_sem=sem,
            recv_sem=sem,
            device_id=target,
            device_id_type=MESH,
        ).wait_send()

    def drain(n):
        gather(n).wait_send()
        sent(pick(n, core_wide, core_narrow), c_send.at[n], sibling)
        sent(pick(n, x_out_wide, x_out_narrow), x_send.at[n], across)
        sent(pick(n, z_out_wide, z_out_narrow), z_send.at[n], {"row": partner(0)})

    near = rows_n // 2
    for place, n in enumerate(order):
        gather(n).wait_recv()
        if n < wides:
            sides = weigh(
                far_wide[n, 0].astype(f32), far_wide[n, 1].astype(f32), mask_wide[1, n // per_super]
            )
        else:
            packed = far_pack[n - wides].astype(f32)
            turned = swap(packed)
            sides = weigh(
                jnp.where(low, packed, turned), jnp.where(low, turned, packed), mask_wide[1, supers - 1]
            )
        for i, side in enumerate(sides):
            high, rest = split(side)
            rows = slice(i * depth, (i + 1) * depth)
            if n < wides:
                rhs_wide[rows, :LANES] = high.astype(bf16)
                rhs_wide[rows, LANES:] = rest.astype(bf16)
            else:
                rhs_narrow[rows, :] = jnp.where(low, high, rest).astype(bf16)
        before = order[place - 1]
        if place < chunks - 1:
            products(n, 0, steps, 2 - rows_n % 2)
            send_x_range(n, 0, rows_n)
            if place:
                send_z_range(before, 0, rows_n if place < chunks - 2 else near)
            if 2 <= place < chunks - 2:
                finish(order[place - 2])
                drain(order[place - 2])
        else:

            def after(i):
                @pl.when(i >= 2)
                def _():
                    send_x(n, i - 2)

            products(n, 0, rows_n, 1, after)
            send_x_range(n, rows_n - 2, 2)
            products(n, rows_n, rows_n, 2 - rows_n % 2)
            for d in range(near, rows_n):
                send_z_range(order[place - 2], d, 1)
            for d in range(rows_n):
                send_z_range(before, d, 1)
            for d in range(rows_n):
                send_z_range(n, d, 1)
    for n in order[-4:-1]:
        finish(n)
    for n in order[-4:-1]:
        drain(n)
    first = sum_narrow[0]
    second = finish(wides + 1)
    keep = low_lanes(owned // 2)
    out_ref[0, 0, : owned // 2, last] = jnp.where(keep, first, swap(second)).astype(bf16)
    out_ref[0, 0, owned // 2 :, last] = jnp.where(keep, swap(first), second).astype(bf16)

    masks.wait_send()
    drain(chunks - 1)


def fused(inverse, factor, block_mask, pole_real, pole_imaginary):
    rows_n = lax.axis_size("row")
    height, width = inverse.shape[2:]
    depth, columns_all = factor.shape[2:]
    wides = columns_all // LANES - 1
    chunks = wides + 2
    owned = height // (rows_n * 4)
    half = owned // 2
    steps = 2 * rows_n
    f32, bf16, i16 = jnp.float32, jnp.bfloat16, jnp.int16
    dma = pltpu.SemaphoreType.DMA
    big = pl.BlockSpec(memory_space=pltpu.HBM)

    def both(lead, rows, kind):
        return [
            pltpu.VMEM((wides,) + lead + (rows[0], LANES), kind),
            pltpu.VMEM((2,) + lead + (rows[1], LANES), kind),
        ]

    full = (owned, half)
    coded = (owned + 16, half + 16)
    return pl.pallas_call(
        functools.partial(kernel, rows_n),
        out_shape=jax.ShapeDtypeStruct((1, 1, owned, columns_all), jnp.bfloat16),
        in_specs=[big] * 5,
        out_specs=pl.BlockSpec(memory_space=pltpu.VMEM),
        scratch_shapes=[
            pltpu.VMEM((height, 2 * depth), bf16),
            pltpu.VMEM((height, 2 * depth), bf16),
            pltpu.VMEM((2, depth, columns_all), bf16),
            pltpu.VMEM((wides, 2, depth, LANES), bf16),
            pltpu.VMEM((2, depth, LANES), bf16),
            pltpu.VMEM((2, depth, LANES), bf16),
            pltpu.SMEM(pole_real.shape, f32),
            pltpu.SMEM(pole_imaginary.shape, f32),
            pltpu.VMEM(block_mask.shape, block_mask.dtype),
            pltpu.VMEM(block_mask.shape, block_mask.dtype),
            pltpu.VMEM((2, block_mask.shape[0], depth, LANES), f32),
            pltpu.VMEM((2 * depth, 2 * columns_all), bf16),
            pltpu.VMEM((2 * depth, 2 * LANES), bf16),
            pltpu.VMEM((2 * depth, LANES), bf16),
            *both((steps, 2), full, f32),
            *both((steps,), full, f32),
            *both((rows_n,), coded, i16),
            *both((rows_n,), coded, i16),
            *both((rows_n - 1,), coded, i16),
            *both((rows_n - 1,), coded, i16),
            *both((), full, f32),
            dma((2, 2, steps)),
            dma((wides + 1,)),
            dma((3,)),
            dma((chunks,)),
            dma((chunks,)),
            dma,
            dma,
            dma((chunks,)),
            dma((chunks, steps)),
            dma((chunks,)),
            dma((chunks, rows_n)),
            dma((chunks,)),
            dma((chunks, rows_n)),
        ],
        compiler_params=pltpu.CompilerParams(
            collective_id=0, has_side_effects=True, vmem_limit_bytes=53 * 1024 * 1024
        ),
    )(pole_real, pole_imaginary, block_mask, factor, inverse)


def solution(mesh):
    sizes = dict(mesh.shape)

    def shards(inverse, factor, block_mask, pole_real, pole_imaginary):
        supers = block_mask.shape[0]
        wide = factor.shape[3] // supers
        small = 2 * inverse.shape[2] * inverse.shape[3] * 2 <= 20 * 1024 * 1024
        fits = sizes["pole"] == 4 and sizes["col"] == 2 and sizes["row"] >= 2
        owned = inverse.shape[2] // (sizes["row"] * 4)
        if fits and small and wide % LANES == 0 and owned % 32 == 0:
            body = fused
        else:
            body = plain
        return body(inverse, factor, block_mask, pole_real, pole_imaginary)

    return jax.shard_map(
        shards,
        mesh=mesh,
        in_specs=(
            P("pole", None, "col", "row"),
            P("pole", None, ("row", "col"), None),
            P(None, ("row", "col")),
            P("pole"),
            P("pole"),
        ),
        out_specs=P("col", "row", "pole", None),
        check_vma=False,
    )
```

```python
import functools

import jax
import jax.numpy as jnp
from jax import lax
from jax.experimental import pallas as pl
from jax.experimental.pallas import tpu as pltpu
from jax.sharding import PartitionSpec as P

W = 256
BLK = 32
LANES = 128
HALF = LANES // 2
TOP = 32000.0
STEPS = 8.0
MESH = pl.DeviceIdType.MESH


def plain(inverse, factor, block_mask, pole_real, pole_imaginary):
    row_mask = jnp.repeat(block_mask.T, BLK, axis=0)
    column_mask = jnp.repeat(row_mask, W, axis=1).astype(jnp.bfloat16)
    masked = factor[0] * column_mask[None]
    inverse_real = inverse[0, 0]
    inverse_imaginary = inverse[0, 1]
    height = inverse_real.shape[0]
    columns_all = masked.shape[2]
    piece = lax.all_gather(masked, "col", axis=1, tiled=True)
    running_real = jnp.dot(inverse_real, piece[0], preferred_element_type=jnp.float32) - jnp.dot(
        inverse_imaginary, piece[1], preferred_element_type=jnp.float32
    )
    running_imaginary = jnp.dot(
        inverse_real, piece[1], preferred_element_type=jnp.float32
    ) + jnp.dot(inverse_imaginary, piece[0], preferred_element_type=jnp.float32)
    weight_real = pole_real[0]
    weight_imaginary = pole_imaginary[0]
    weighted = weight_real * running_real - weight_imaginary * running_imaginary
    row_count = lax.axis_size("row")
    pole_count = lax.axis_size("pole")
    owned = height // (row_count * pole_count)
    reordered = (
        weighted.reshape(row_count, pole_count, owned, columns_all)
        .transpose(1, 0, 2, 3)
        .reshape(height, columns_all)
    )
    density = lax.psum_scatter(reordered, ("pole", "row"), scatter_dimension=0, tiled=True)
    return density.reshape(1, 1, density.shape[0], columns_all).astype(jnp.bfloat16)


def spread(blocks_mask, depth):
    supers, blocks = blocks_mask.shape
    values = blocks_mask.astype(jnp.float32)
    row = lax.broadcasted_iota(jnp.int32, (depth, blocks), 0)
    block = lax.broadcasted_iota(jnp.int32, (depth, blocks), 1)
    low = block * (depth // blocks)
    inside = jnp.logical_and(row >= low, row < low + depth // blocks)
    columns = []
    for s in range(supers):
        chosen = jnp.where(inside, values[s : s + 1, :], 0.0)
        column = jnp.sum(chosen, axis=1, keepdims=True)
        columns.append(jnp.broadcast_to(column, (depth, LANES)))
    return columns


def low_lanes(rows):
    return lax.broadcasted_iota(jnp.int32, (rows, LANES), 1) < HALF


def swap(value):
    return pltpu.roll(value, HALF, 1)


def split(value):
    high = value.astype(jnp.bfloat16).astype(jnp.float32)
    return high, value - high


def encode(value, ref):
    rows = value.shape[0]
    largest = jnp.max(jnp.abs(value), axis=0, keepdims=True)
    level = jnp.ceil(jnp.log2(jnp.maximum(largest, 1e-30)) * STEPS)
    scaled = value * (TOP * jnp.exp2(level * (-1.0 / STEPS)))
    magic = 12582912.0
    whole = (scaled + magic) - magic
    ref[0:rows, :] = whole.astype(jnp.int32).astype(jnp.int16)
    wide = jnp.broadcast_to(level, (16, LANES))
    ref[rows : rows + 16, :] = wide.astype(jnp.int32).astype(jnp.int16)


def decode(ref):
    rows = ref.shape[0] - 16
    level = ref[rows : rows + 16, :].astype(jnp.int32).astype(jnp.float32)[0:1, :]
    scale = jnp.exp2(level * (1.0 / STEPS)) * (1.0 / TOP)
    return ref[0:rows, :].astype(jnp.int32).astype(jnp.float32) * scale


def kernel(
    rows_n,
    real_hbm,
    imaginary_hbm,
    mask_hbm,
    factor_ref,
    inverse_ref,
    out_ref,
    a_own,
    a_far,
    own_f,
    far_wide,
    pack,
    far_pack,
    real_ref,
    imaginary_ref,
    mask_ref,
    far_mask,
    mask_wide,
    rhs_own,
    rhs_wide,
    rhs_narrow,
    part_wide,
    part_narrow,
    core_wide,
    core_narrow,
    x_out_wide,
    x_out_narrow,
    x_in_wide,
    x_in_narrow,
    z_out_wide,
    z_out_narrow,
    z_in_wide,
    z_in_narrow,
    sum_wide,
    sum_narrow,
    load_sem,
    own_sem,
    small_sem,
    y_send,
    y_recv,
    m_send,
    m_recv,
    c_send,
    c_recv,
    x_send,
    x_recv,
    z_send,
    z_recv,
):
    p = lax.axis_index("pole")
    z = lax.axis_index("row")
    y = lax.axis_index("col")
    core = lax.rem(p, 2)
    x = p // 2
    sibling = {"pole": x * 2 + 1 - core}
    across = {"pole": (1 - x) * 2 + core}
    beside = {"col": 1 - y}
    depth = factor_ref.shape[2]
    wides = far_wide.shape[0]
    chunks = wides + 2
    owned = out_ref.shape[2]
    pair = 2 * owned
    group = 4 * owned
    supers = mask_ref.shape[0]
    per_super = (wides + 1) // supers
    steps = 2 * rows_n
    f32 = jnp.float32
    bf16 = jnp.bfloat16

    order = list(range(chunks))

    barrier = pltpu.get_barrier_semaphore()
    pl.semaphore_signal(barrier, inc=1, device_id=sibling, device_id_type=MESH)
    pl.semaphore_signal(barrier, inc=1, device_id=across, device_id_type=MESH)
    pl.semaphore_signal(barrier, inc=1, device_id=beside, device_id_type=MESH)
    for d in range(1, rows_n):
        pl.semaphore_signal(
            barrier, inc=1, device_id={"row": lax.rem(z + d, rows_n)}, device_id_type=MESH
        )

    def partner(j):
        step = rows_n - 1 - j
        if rows_n & (rows_n - 1):
            return lax.rem(z + rows_n - step, rows_n)
        other = 0
        bit = 1
        while bit < rows_n:
            other = other + bit * lax.rem(z // bit + step // bit, 2)
            bit *= 2
        return other

    def load(far, which, j):
        r = partner(lax.rem(j, rows_n))
        h = jnp.where(j < rows_n, 1 - x, x)
        rows = pl.ds(pl.multiple_of(r * group + h * pair, pair), pair)
        side = (1 - y) if far else y
        columns = pl.ds(pl.multiple_of(side * depth, depth), depth)
        target = a_far if far else a_own
        return pltpu.make_async_copy(
            inverse_ref.at[0, which, rows, columns],
            target.at[pl.ds(pl.multiple_of(j * pair, pair), pair), which * depth : (which + 1) * depth],
            load_sem.at[far, which, j],
        )

    def own_copy(n):
        columns = pl.ds(n * LANES, LANES)
        return pltpu.make_async_copy(
            factor_ref.at[0, :, :, columns], own_f.at[:, :, columns], own_sem.at[n]
        )

    def gather(n):
        if n < wides:
            source, target = own_f.at[:, :, pl.ds(n * LANES, LANES)], far_wide.at[n]
        else:
            source, target = pack.at[n - wides], far_pack.at[n - wides]
        return pltpu.make_async_remote_copy(
            src_ref=source,
            dst_ref=target,
            send_sem=y_send.at[n],
            recv_sem=y_recv.at[n],
            device_id=beside,
            device_id_type=MESH,
        )

    masks = pltpu.make_async_remote_copy(
        src_ref=mask_hbm,
        dst_ref=far_mask,
        send_sem=m_send,
        recv_sem=m_recv,
        device_id=beside,
        device_id_type=MESH,
    )

    def pick(n, wide, narrow):
        return wide.at[n] if n < wides else narrow.at[n - wides]

    def core_copy(n, j):
        return pltpu.make_async_remote_copy(
            src_ref=pick(n, part_wide, part_narrow).at[j, 1 - core],
            dst_ref=pick(n, core_wide, core_narrow).at[j],
            send_sem=c_send.at[n],
            recv_sem=c_recv.at[n, j],
            device_id=sibling,
            device_id_type=MESH,
        )

    def x_copy(n, j):
        return pltpu.make_async_remote_copy(
            src_ref=pick(n, x_out_wide, x_out_narrow).at[j],
            dst_ref=pick(n, x_in_wide, x_in_narrow).at[j],
            send_sem=x_send.at[n],
            recv_sem=x_recv.at[n, j],
            device_id=across,
            device_id_type=MESH,
        )

    def z_copy(n, d):
        return pltpu.make_async_remote_copy(
            src_ref=pick(n, z_out_wide, z_out_narrow).at[d],
            dst_ref=pick(n, z_in_wide, z_in_narrow).at[d],
            send_sem=z_send.at[n],
            recv_sem=z_recv.at[n, d],
            device_id={"row": partner(d)},
            device_id_type=MESH,
        )

    small = [
        pltpu.make_async_copy(source, target, small_sem.at[i])
        for i, (source, target) in enumerate(
            ((mask_hbm, mask_ref), (real_hbm, real_ref), (imaginary_hbm, imaginary_ref))
        )
    ]
    for n in range(wides + 1):
        own_copy(n).start()

    def load_all(far):
        def body(j, carry):
            load(far, 0, j).start()
            load(far, 1, j).start()
            return carry

        lax.fori_loop(0, steps, body, 0)

    pl.semaphore_wait(barrier, 3 + rows_n - 1)
    own_copy(0).wait()
    gather(0).start()
    masks.start()
    for copy in small:
        copy.start()
    load_all(0)
    for n in range(1, wides + 1):
        own_copy(n).wait()

    last = slice(wides * LANES, (wides + 1) * LANES)
    low = low_lanes(depth)
    real_last = own_f[0, :, last].astype(f32)
    imaginary_last = own_f[1, :, last].astype(f32)
    pack[0] = jnp.where(low, real_last, swap(imaginary_last)).astype(bf16)
    pack[1] = jnp.where(low, swap(real_last), imaginary_last).astype(bf16)
    for n in order[1:]:
        gather(n).start()
    load_all(1)

    for copy in small:
        copy.wait()
    weight_real = real_ref[0]
    weight_imaginary = imaginary_ref[0]
    for s, column in enumerate(spread(mask_ref[...], depth)):
        mask_wide[0, s] = column

    def weigh(real, imaginary, mask):
        first = (weight_real * real - weight_imaginary * imaginary) * mask
        second = (weight_real * imaginary + weight_imaginary * real) * (-mask)
        return first, second

    for n in range(wides + 1):
        columns = slice(n * LANES, (n + 1) * LANES)
        sides = weigh(
            own_f[0, :, columns].astype(f32), own_f[1, :, columns].astype(f32), mask_wide[0, n // per_super]
        )
        for i, side in enumerate(sides):
            high, rest = split(side)
            if n == wides:
                high, rest = jnp.where(low, high, swap(rest)), jnp.where(low, swap(high), rest)
            rows = slice(i * depth, (i + 1) * depth)
            rhs_own[rows, 2 * n * LANES : (2 * n + 1) * LANES] = high.astype(bf16)
            rhs_own[rows, (2 * n + 1) * LANES : (2 * n + 2) * LANES] = rest.astype(bf16)

    def fold_wide(value):
        return (value[:, :LANES] + value[:, LANES:]).reshape(2, owned, LANES)

    def fold_narrow(value):
        both = value + swap(value)
        both = both.reshape(4, owned // 2, LANES)
        keep = low_lanes(owned // 2)
        return [jnp.where(keep, both[2 * c], both[2 * c + 1]) for c in range(2)]

    def block(j):
        return pl.ds(pl.multiple_of(j * pair, pair), pair)

    def own_body(j, carry):
        load(0, 0, j).wait()
        load(0, 1, j).wait()
        value = jnp.dot(a_own[block(j), :], rhs_own[...], preferred_element_type=f32)
        for n in range(wides):
            part_wide[n, j] = fold_wide(value[:, 2 * n * LANES : (2 * n + 2) * LANES])
        for k in range(2):
            low_column = (2 * wides + k) * LANES
            folded = fold_narrow(value[:, low_column : low_column + LANES])
            for c in range(2):
                part_narrow[k, j, c] = folded[c]
        return carry

    lax.fori_loop(0, steps, own_body, 0)
    masks.wait_recv()
    for s, column in enumerate(spread(far_mask[...], depth)):
        mask_wide[1, s] = column

    def send_x(n, j):
        core_copy(n, j).wait_recv()
        total = pick(n, part_wide, part_narrow)[j, core] + pick(n, core_wide, core_narrow)[j]
        encode(total, pick(n, x_out_wide, x_out_narrow).at[j])
        x_copy(n, j).start()

    def finish(n):
        total = pick(n, sum_wide, sum_narrow)[...]
        for d in range(rows_n - 1):
            z_copy(n, d).wait_recv()
        for d in range(rows_n - 1):
            total = total + decode(pick(n, z_in_wide, z_in_narrow).at[d])
        if n < wides:
            out_ref[0, 0, :, n * LANES : (n + 1) * LANES] = total.astype(bf16)
        else:
            sum_narrow[n - wides] = total
        return total

    def products(n, first, count, per, after=None):
        def body(i, carry):
            begin = first + i * per
            right = rhs_wide[...] if n < wides else rhs_narrow[...]
            for k in range(per):
                j = begin + k
                if n == 0:
                    load(1, 0, j).wait()
                    load(1, 1, j).wait()
            for k in range(per):
                j = begin + k
                value = jnp.dot(a_far[block(j), :], right, preferred_element_type=f32)
                if n < wides:
                    part_wide[n, j] += fold_wide(value)
                else:
                    folded = fold_narrow(value)
                    for c in range(2):
                        part_narrow[n - wides, j, c] += folded[c]
            for k in range(per):
                core_copy(n, begin + k).start()
            if after is not None:
                after(i)
            return carry

        lax.fori_loop(0, count // per, body, 0)

    def send_x_range(n, first, count):
        for j in range(first, first + count):
            core_copy(n, j).wait_recv()
        for j in range(first, first + count):
            total = pick(n, part_wide, part_narrow)[j, core] + pick(n, core_wide, core_narrow)[j]
            encode(total, pick(n, x_out_wide, x_out_narrow).at[j])
        for j in range(first, first + count):
            x_copy(n, j).start()

    def send_z_range(n, first, count):
        chosen = range(first, first + count)
        for d in chosen:
            core_copy(n, d + rows_n).wait_recv()
            x_copy(n, d).wait_recv()
        for d in chosen:
            j = d + rows_n
            total = pick(n, part_wide, part_narrow)[j, core] + pick(n, core_wide, core_narrow)[j]
            total = total + decode(pick(n, x_in_wide, x_in_narrow).at[d])
            if d < rows_n - 1:
                encode(total, pick(n, z_out_wide, z_out_narrow).at[d])
            else:
                pick(n, sum_wide, sum_narrow)[...] = total
        for d in chosen:
            if d < rows_n - 1:
                z_copy(n, d).start()

    def sent(source, sem, target):
        pltpu.make_async_remote_copy(
            src_ref=source,
            dst_ref=source,
            send_sem=sem,
            recv_sem=sem,
            device_id=target,
            device_id_type=MESH,
        ).wait_send()

    def drain(n):
        gather(n).wait_send()
        sent(pick(n, core_wide, core_narrow), c_send.at[n], sibling)
        sent(pick(n, x_out_wide, x_out_narrow), x_send.at[n], across)
        sent(pick(n, z_out_wide, z_out_narrow), z_send.at[n], {"row": partner(0)})

    near = rows_n // 2
    for place, n in enumerate(order):
        gather(n).wait_recv()
        if n < wides:
            sides = weigh(
                far_wide[n, 0].astype(f32), far_wide[n, 1].astype(f32), mask_wide[1, n // per_super]
            )
        else:
            packed = far_pack[n - wides].astype(f32)
            turned = swap(packed)
            sides = weigh(
                jnp.where(low, packed, turned), jnp.where(low, turned, packed), mask_wide[1, supers - 1]
            )
        for i, side in enumerate(sides):
            high, rest = split(side)
            rows = slice(i * depth, (i + 1) * depth)
            if n < wides:
                rhs_wide[rows, :LANES] = high.astype(bf16)
                rhs_wide[rows, LANES:] = rest.astype(bf16)
            else:
                rhs_narrow[rows, :] = jnp.where(low, high, rest).astype(bf16)
        before = order[place - 1]
        if place < chunks - 1:
            per = 2 - rows_n % 2
            lag = 2

            def after_part(i):
                for k in range(rows_n // per):

                    @pl.when(i == k + lag)
                    def _():
                        send_x_range(n, k * per, per)

            products(n, 0, steps, per, after_part)
            if place:
                for d in range(rows_n if place < chunks - 2 else near):
                    send_z_range(before, d, 1)
            if 2 <= place < chunks - 2:
                finish(order[place - 2])
                drain(order[place - 2])
        else:

            def after_own(i):
                for k in range(rows_n // per):

                    @pl.when(i == k)
                    def _():
                        send_z_range(before, k + 1, 1)

            products(n, 0, rows_n, per)
            send_x_range(n, 0, 1)
            send_x_range(n, 1, 1)
            for d in range(near, rows_n - 1):
                send_z_range(order[place - 2], d, 1)
            for k in range(rows_n - 2, rows_n):
                send_x_range(n, k, 1)
            send_z_range(before, 0, 1)
            products(n, rows_n, rows_n, per, after_own)
            for d in range(rows_n // per + 1, rows_n):
                send_z_range(before, d, 1)
            send_z_range(order[place - 2], rows_n - 1, 1)
            for d in range(rows_n):
                send_z_range(n, d, 1)
    for n in order[-4:-1]:
        finish(n)
    for n in order[-4:-1]:
        drain(n)
    first = sum_narrow[0]
    second = finish(wides + 1)
    keep = low_lanes(owned // 2)
    out_ref[0, 0, : owned // 2, last] = jnp.where(keep, first, swap(second)).astype(bf16)
    out_ref[0, 0, owned // 2 :, last] = jnp.where(keep, swap(first), second).astype(bf16)

    masks.wait_send()
    drain(chunks - 1)


def fused(inverse, factor, block_mask, pole_real, pole_imaginary):
    rows_n = lax.axis_size("row")
    height, width = inverse.shape[2:]
    depth, columns_all = factor.shape[2:]
    wides = columns_all // LANES - 1
    chunks = wides + 2
    owned = height // (rows_n * 4)
    half = owned // 2
    steps = 2 * rows_n
    f32, bf16, i16 = jnp.float32, jnp.bfloat16, jnp.int16
    dma = pltpu.SemaphoreType.DMA
    big = pl.BlockSpec(memory_space=pltpu.HBM)

    def both(lead, rows, kind):
        return [
            pltpu.VMEM((wides,) + lead + (rows[0], LANES), kind),
            pltpu.VMEM((2,) + lead + (rows[1], LANES), kind),
        ]

    full = (owned, half)
    coded = (owned + 16, half + 16)
    return pl.pallas_call(
        functools.partial(kernel, rows_n),
        out_shape=jax.ShapeDtypeStruct((1, 1, owned, columns_all), jnp.bfloat16),
        in_specs=[big] * 5,
        out_specs=pl.BlockSpec(memory_space=pltpu.VMEM),
        scratch_shapes=[
            pltpu.VMEM((height, 2 * depth), bf16),
            pltpu.VMEM((height, 2 * depth), bf16),
            pltpu.VMEM((2, depth, columns_all), bf16),
            pltpu.VMEM((wides, 2, depth, LANES), bf16),
            pltpu.VMEM((2, depth, LANES), bf16),
            pltpu.VMEM((2, depth, LANES), bf16),
            pltpu.SMEM(pole_real.shape, f32),
            pltpu.SMEM(pole_imaginary.shape, f32),
            pltpu.VMEM(block_mask.shape, block_mask.dtype),
            pltpu.VMEM(block_mask.shape, block_mask.dtype),
            pltpu.VMEM((2, block_mask.shape[0], depth, LANES), f32),
            pltpu.VMEM((2 * depth, 2 * columns_all), bf16),
            pltpu.VMEM((2 * depth, 2 * LANES), bf16),
            pltpu.VMEM((2 * depth, LANES), bf16),
            *both((steps, 2), full, f32),
            *both((steps,), full, f32),
            *both((rows_n,), coded, i16),
            *both((rows_n,), coded, i16),
            *both((rows_n - 1,), coded, i16),
            *both((rows_n - 1,), coded, i16),
            *both((), full, f32),
            dma((2, 2, steps)),
            dma((wides + 1,)),
            dma((3,)),
            dma((chunks,)),
            dma((chunks,)),
            dma,
            dma,
            dma((chunks,)),
            dma((chunks, steps)),
            dma((chunks,)),
            dma((chunks, rows_n)),
            dma((chunks,)),
            dma((chunks, rows_n)),
        ],
        compiler_params=pltpu.CompilerParams(
            collective_id=0, has_side_effects=True, vmem_limit_bytes=53 * 1024 * 1024
        ),
    )(pole_real, pole_imaginary, block_mask, factor, inverse)


def solution(mesh):
    sizes = dict(mesh.shape)

    def shards(inverse, factor, block_mask, pole_real, pole_imaginary):
        supers = block_mask.shape[0]
        wide = factor.shape[3] // supers
        small = 2 * inverse.shape[2] * inverse.shape[3] * 2 <= 20 * 1024 * 1024
        fits = sizes["pole"] == 4 and sizes["col"] == 2 and sizes["row"] >= 2
        owned = inverse.shape[2] // (sizes["row"] * 4)
        if fits and small and wide % LANES == 0 and owned % 32 == 0:
            body = fused
        else:
            body = plain
        return body(inverse, factor, block_mask, pole_real, pole_imaginary)

    return jax.shard_map(
        shards,
        mesh=mesh,
        in_specs=(
            P("pole", None, "col", "row"),
            P("pole", None, ("row", "col"), None),
            P(None, ("row", "col")),
            P("pole"),
            P("pole"),
        ),
        out_specs=P("col", "row", "pole", None),
        check_vma=False,
    )
```

```python
import functools

import jax
import jax.numpy as jnp
from jax import lax
from jax.experimental import pallas as pl
from jax.experimental.pallas import tpu as pltpu
from jax.sharding import PartitionSpec as P

W = 256
BLK = 32
LANES = 128
HALF = LANES // 2
TOP = 32000.0
STEPS = 8.0
MESH = pl.DeviceIdType.MESH


def plain(inverse, factor, block_mask, pole_real, pole_imaginary):
    row_mask = jnp.repeat(block_mask.T, BLK, axis=0)
    column_mask = jnp.repeat(row_mask, W, axis=1).astype(jnp.bfloat16)
    masked = factor[0] * column_mask[None]
    inverse_real = inverse[0, 0]
    inverse_imaginary = inverse[0, 1]
    height = inverse_real.shape[0]
    columns_all = masked.shape[2]
    piece = lax.all_gather(masked, "col", axis=1, tiled=True)
    running_real = jnp.dot(inverse_real, piece[0], preferred_element_type=jnp.float32) - jnp.dot(
        inverse_imaginary, piece[1], preferred_element_type=jnp.float32
    )
    running_imaginary = jnp.dot(
        inverse_real, piece[1], preferred_element_type=jnp.float32
    ) + jnp.dot(inverse_imaginary, piece[0], preferred_element_type=jnp.float32)
    weight_real = pole_real[0]
    weight_imaginary = pole_imaginary[0]
    weighted = weight_real * running_real - weight_imaginary * running_imaginary
    row_count = lax.axis_size("row")
    pole_count = lax.axis_size("pole")
    owned = height // (row_count * pole_count)
    reordered = (
        weighted.reshape(row_count, pole_count, owned, columns_all)
        .transpose(1, 0, 2, 3)
        .reshape(height, columns_all)
    )
    density = lax.psum_scatter(reordered, ("pole", "row"), scatter_dimension=0, tiled=True)
    return density.reshape(1, 1, density.shape[0], columns_all).astype(jnp.bfloat16)


def spread(blocks_mask, depth):
    supers, blocks = blocks_mask.shape
    values = blocks_mask.astype(jnp.float32)
    row = lax.broadcasted_iota(jnp.int32, (depth, blocks), 0)
    block = lax.broadcasted_iota(jnp.int32, (depth, blocks), 1)
    low = block * (depth // blocks)
    inside = jnp.logical_and(row >= low, row < low + depth // blocks)
    columns = []
    for s in range(supers):
        chosen = jnp.where(inside, values[s : s + 1, :], 0.0)
        column = jnp.sum(chosen, axis=1, keepdims=True)
        columns.append(jnp.broadcast_to(column, (depth, LANES)))
    return columns


def low_lanes(rows):
    return lax.broadcasted_iota(jnp.int32, (rows, LANES), 1) < HALF


def swap(value):
    return pltpu.roll(value, HALF, 1)


def split(value):
    high = value.astype(jnp.bfloat16).astype(jnp.float32)
    return high, value - high


def encode(value, ref):
    rows = value.shape[0]
    largest = jnp.max(jnp.abs(value), axis=0, keepdims=True)
    level = jnp.ceil(jnp.log2(jnp.maximum(largest, 1e-30)) * STEPS)
    scaled = value * (TOP * jnp.exp2(level * (-1.0 / STEPS)))
    magic = 12582912.0
    whole = (scaled + magic) - magic
    ref[0:rows, :] = whole.astype(jnp.int32).astype(jnp.int16)
    wide = jnp.broadcast_to(level, (16, LANES))
    ref[rows : rows + 16, :] = wide.astype(jnp.int32).astype(jnp.int16)


def decode(ref):
    rows = ref.shape[0] - 16
    level = ref[rows : rows + 16, :].astype(jnp.int32).astype(jnp.float32)[0:1, :]
    scale = jnp.exp2(level * (1.0 / STEPS)) * (1.0 / TOP)
    return ref[0:rows, :].astype(jnp.int32).astype(jnp.float32) * scale


def kernel(
    rows_n,
    real_hbm,
    imaginary_hbm,
    mask_hbm,
    factor_ref,
    inverse_ref,
    out_ref,
    a_own,
    a_far,
    own_f,
    far_wide,
    pack,
    far_pack,
    real_ref,
    imaginary_ref,
    mask_ref,
    far_mask,
    mask_wide,
    rhs_own,
    rhs_wide,
    rhs_narrow,
    part_wide,
    part_narrow,
    core_wide,
    core_narrow,
    x_out_wide,
    x_out_narrow,
    x_in_wide,
    x_in_narrow,
    z_out_wide,
    z_out_narrow,
    z_in_wide,
    z_in_narrow,
    sum_wide,
    sum_narrow,
    load_sem,
    own_sem,
    small_sem,
    y_send,
    y_recv,
    m_send,
    m_recv,
    c_send,
    c_recv,
    x_send,
    x_recv,
    z_send,
    z_recv,
):
    p = lax.axis_index("pole")
    z = lax.axis_index("row")
    y = lax.axis_index("col")
    core = lax.rem(p, 2)
    x = p // 2
    sibling = {"pole": x * 2 + 1 - core}
    across = {"pole": (1 - x) * 2 + core}
    beside = {"col": 1 - y}
    depth = factor_ref.shape[2]
    wides = far_wide.shape[0]
    chunks = wides + 2
    owned = out_ref.shape[2]
    pair = 2 * owned
    group = 4 * owned
    supers = mask_ref.shape[0]
    per_super = (wides + 1) // supers
    steps = 2 * rows_n
    f32 = jnp.float32
    bf16 = jnp.bfloat16

    order = list(range(chunks))

    barrier = pltpu.get_barrier_semaphore()
    pl.semaphore_signal(barrier, inc=1, device_id=sibling, device_id_type=MESH)
    pl.semaphore_signal(barrier, inc=1, device_id=across, device_id_type=MESH)
    pl.semaphore_signal(barrier, inc=1, device_id=beside, device_id_type=MESH)
    for d in range(1, rows_n):
        pl.semaphore_signal(
            barrier, inc=1, device_id={"row": lax.rem(z + d, rows_n)}, device_id_type=MESH
        )

    def partner(j):
        step = rows_n - 1 - j
        if rows_n & (rows_n - 1):
            return lax.rem(z + rows_n - step, rows_n)
        other = 0
        bit = 1
        while bit < rows_n:
            other = other + bit * lax.rem(z // bit + step // bit, 2)
            bit *= 2
        return other

    def load(far, which, j):
        r = partner(lax.rem(j, rows_n))
        h = jnp.where(j < rows_n, 1 - x, x)
        rows = pl.ds(pl.multiple_of(r * group + h * pair, pair), pair)
        side = (1 - y) if far else y
        columns = pl.ds(pl.multiple_of(side * depth, depth), depth)
        target = a_far if far else a_own
        return pltpu.make_async_copy(
            inverse_ref.at[0, which, rows, columns],
            target.at[pl.ds(pl.multiple_of(j * pair, pair), pair), which * depth : (which + 1) * depth],
            load_sem.at[far, which, j],
        )

    def own_copy(n):
        columns = pl.ds(n * LANES, LANES)
        return pltpu.make_async_copy(
            factor_ref.at[0, :, :, columns], own_f.at[:, :, columns], own_sem.at[n]
        )

    def gather(n):
        if n < wides:
            source, target = own_f.at[:, :, pl.ds(n * LANES, LANES)], far_wide.at[n]
        else:
            source, target = pack.at[n - wides], far_pack.at[n - wides]
        return pltpu.make_async_remote_copy(
            src_ref=source,
            dst_ref=target,
            send_sem=y_send.at[n],
            recv_sem=y_recv.at[n],
            device_id=beside,
            device_id_type=MESH,
        )

    masks = pltpu.make_async_remote_copy(
        src_ref=mask_hbm,
        dst_ref=far_mask,
        send_sem=m_send,
        recv_sem=m_recv,
        device_id=beside,
        device_id_type=MESH,
    )

    def pick(n, wide, narrow):
        return wide.at[n] if n < wides else narrow.at[n - wides]

    def core_copy(n, j):
        return pltpu.make_async_remote_copy(
            src_ref=pick(n, part_wide, part_narrow).at[j, 1 - core],
            dst_ref=pick(n, core_wide, core_narrow).at[j],
            send_sem=c_send.at[n],
            recv_sem=c_recv.at[n, j],
            device_id=sibling,
            device_id_type=MESH,
        )

    def x_copy(n, j):
        return pltpu.make_async_remote_copy(
            src_ref=pick(n, x_out_wide, x_out_narrow).at[j],
            dst_ref=pick(n, x_in_wide, x_in_narrow).at[j],
            send_sem=x_send.at[n],
            recv_sem=x_recv.at[n, j],
            device_id=across,
            device_id_type=MESH,
        )

    def z_copy(n, d):
        return pltpu.make_async_remote_copy(
            src_ref=pick(n, z_out_wide, z_out_narrow).at[d],
            dst_ref=pick(n, z_in_wide, z_in_narrow).at[d],
            send_sem=z_send.at[n],
            recv_sem=z_recv.at[n, d],
            device_id={"row": partner(d)},
            device_id_type=MESH,
        )

    small = [
        pltpu.make_async_copy(source, target, small_sem.at[i])
        for i, (source, target) in enumerate(
            ((mask_hbm, mask_ref), (real_hbm, real_ref), (imaginary_hbm, imaginary_ref))
        )
    ]
    for n in range(wides + 1):
        own_copy(n).start()

    def load_all(far):
        def body(j, carry):
            load(far, 0, j).start()
            load(far, 1, j).start()
            return carry

        lax.fori_loop(0, steps, body, 0)

    pl.semaphore_wait(barrier, 3 + rows_n - 1)
    own_copy(0).wait()
    gather(0).start()
    masks.start()
    for copy in small:
        copy.start()
    load_all(0)
    for n in range(1, wides + 1):
        own_copy(n).wait()

    last = slice(wides * LANES, (wides + 1) * LANES)
    low = low_lanes(depth)
    real_last = own_f[0, :, last].astype(f32)
    imaginary_last = own_f[1, :, last].astype(f32)
    pack[0] = jnp.where(low, real_last, swap(imaginary_last)).astype(bf16)
    pack[1] = jnp.where(low, swap(real_last), imaginary_last).astype(bf16)
    for n in order[1:]:
        gather(n).start()
    load_all(1)

    for copy in small:
        copy.wait()
    weight_real = real_ref[0]
    weight_imaginary = imaginary_ref[0]
    for s, column in enumerate(spread(mask_ref[...], depth)):
        mask_wide[0, s] = column

    def weigh(real, imaginary, mask):
        first = (weight_real * real - weight_imaginary * imaginary) * mask
        second = (weight_real * imaginary + weight_imaginary * real) * (-mask)
        return first, second

    for n in range(wides + 1):
        columns = slice(n * LANES, (n + 1) * LANES)
        sides = weigh(
            own_f[0, :, columns].astype(f32), own_f[1, :, columns].astype(f32), mask_wide[0, n // per_super]
        )
        for i, side in enumerate(sides):
            high, rest = split(side)
            if n == wides:
                high, rest = jnp.where(low, high, swap(rest)), jnp.where(low, swap(high), rest)
            rows = slice(i * depth, (i + 1) * depth)
            rhs_own[rows, 2 * n * LANES : (2 * n + 1) * LANES] = high.astype(bf16)
            rhs_own[rows, (2 * n + 1) * LANES : (2 * n + 2) * LANES] = rest.astype(bf16)

    def fold_wide(value):
        return (value[:, :LANES] + value[:, LANES:]).reshape(2, owned, LANES)

    def fold_narrow(value):
        both = value + swap(value)
        both = both.reshape(4, owned // 2, LANES)
        keep = low_lanes(owned // 2)
        return [jnp.where(keep, both[2 * c], both[2 * c + 1]) for c in range(2)]

    def block(j):
        return pl.ds(pl.multiple_of(j * pair, pair), pair)

    def own_body(j, carry):
        load(0, 0, j).wait()
        load(0, 1, j).wait()
        value = jnp.dot(a_own[block(j), :], rhs_own[...], preferred_element_type=f32)
        for n in range(wides):
            part_wide[n, j] = fold_wide(value[:, 2 * n * LANES : (2 * n + 2) * LANES])
        for k in range(2):
            low_column = (2 * wides + k) * LANES
            folded = fold_narrow(value[:, low_column : low_column + LANES])
            for c in range(2):
                part_narrow[k, j, c] = folded[c]
        return carry

    lax.fori_loop(0, steps, own_body, 0)
    masks.wait_recv()
    for s, column in enumerate(spread(far_mask[...], depth)):
        mask_wide[1, s] = column

    def send_x(n, j):
        core_copy(n, j).wait_recv()
        total = pick(n, part_wide, part_narrow)[j, core] + pick(n, core_wide, core_narrow)[j]
        encode(total, pick(n, x_out_wide, x_out_narrow).at[j])
        x_copy(n, j).start()

    def finish(n):
        total = pick(n, sum_wide, sum_narrow)[...]
        for d in range(rows_n - 1):
            z_copy(n, d).wait_recv()
        for d in range(rows_n - 1):
            total = total + decode(pick(n, z_in_wide, z_in_narrow).at[d])
        if n < wides:
            out_ref[0, 0, :, n * LANES : (n + 1) * LANES] = total.astype(bf16)
        else:
            sum_narrow[n - wides] = total
        return total

    def products(n, first, count, per, after=None):
        def body(i, carry):
            begin = first + i * per
            right = rhs_wide[...] if n < wides else rhs_narrow[...]
            for k in range(per):
                j = begin + k
                if n == 0:
                    load(1, 0, j).wait()
                    load(1, 1, j).wait()
            for k in range(per):
                j = begin + k
                value = jnp.dot(a_far[block(j), :], right, preferred_element_type=f32)
                if n < wides:
                    part_wide[n, j] += fold_wide(value)
                else:
                    folded = fold_narrow(value)
                    for c in range(2):
                        part_narrow[n - wides, j, c] += folded[c]
            for k in range(per):
                core_copy(n, begin + k).start()
            if after is not None:
                after(i)
            return carry

        lax.fori_loop(0, count // per, body, 0)

    def send_x_range(n, first, count):
        for j in range(first, first + count):
            core_copy(n, j).wait_recv()
        for j in range(first, first + count):
            total = pick(n, part_wide, part_narrow)[j, core] + pick(n, core_wide, core_narrow)[j]
            encode(total, pick(n, x_out_wide, x_out_narrow).at[j])
        for j in range(first, first + count):
            x_copy(n, j).start()

    def send_z_range(n, first, count):
        chosen = range(first, first + count)
        for d in chosen:
            core_copy(n, d + rows_n).wait_recv()
            x_copy(n, d).wait_recv()
        for d in chosen:
            j = d + rows_n
            total = pick(n, part_wide, part_narrow)[j, core] + pick(n, core_wide, core_narrow)[j]
            total = total + decode(pick(n, x_in_wide, x_in_narrow).at[d])
            if d < rows_n - 1:
                encode(total, pick(n, z_out_wide, z_out_narrow).at[d])
            else:
                pick(n, sum_wide, sum_narrow)[...] = total
        for d in chosen:
            if d < rows_n - 1:
                z_copy(n, d).start()

    def sent(source, sem, target):
        pltpu.make_async_remote_copy(
            src_ref=source,
            dst_ref=source,
            send_sem=sem,
            recv_sem=sem,
            device_id=target,
            device_id_type=MESH,
        ).wait_send()

    def drain(n):
        gather(n).wait_send()
        sent(pick(n, core_wide, core_narrow), c_send.at[n], sibling)
        sent(pick(n, x_out_wide, x_out_narrow), x_send.at[n], across)
        sent(pick(n, z_out_wide, z_out_narrow), z_send.at[n], {"row": partner(0)})

    near = rows_n // 2
    for place, n in enumerate(order):
        gather(n).wait_recv()
        if n < wides:
            sides = weigh(
                far_wide[n, 0].astype(f32), far_wide[n, 1].astype(f32), mask_wide[1, n // per_super]
            )
        else:
            packed = far_pack[n - wides].astype(f32)
            turned = swap(packed)
            sides = weigh(
                jnp.where(low, packed, turned), jnp.where(low, turned, packed), mask_wide[1, supers - 1]
            )
        for i, side in enumerate(sides):
            high, rest = split(side)
            rows = slice(i * depth, (i + 1) * depth)
            if n < wides:
                rhs_wide[rows, :LANES] = high.astype(bf16)
                rhs_wide[rows, LANES:] = rest.astype(bf16)
            else:
                rhs_narrow[rows, :] = jnp.where(low, high, rest).astype(bf16)
        before = order[place - 1]
        if place < chunks - 1:
            per = rows_n if place == chunks - 2 else 2 - rows_n % 2
            lag = 1 if place == chunks - 2 else 2

            def after_part(i):
                for k in range(rows_n // per):

                    @pl.when(i == k + lag)
                    def _():
                        send_x_range(n, k * per, per)

            products(n, 0, steps, per, after_part)
            if place:
                for d in range(rows_n if place < chunks - 2 else near):
                    send_z_range(before, d, 1)
            if 2 <= place < chunks - 2:
                finish(order[place - 2])
                drain(order[place - 2])
        else:
            per = 2 - rows_n % 2

            def after_own(i):
                for k in range(rows_n // per):

                    @pl.when(i == k)
                    def _():
                        send_z_range(before, k + 1, 1)

            products(n, 0, rows_n, per)
            send_x_range(n, 0, 1)
            send_x_range(n, 1, 1)
            for d in range(near, rows_n - 1):
                send_z_range(order[place - 2], d, 1)
            for k in range(rows_n - 2, rows_n):
                send_x_range(n, k, 1)
            send_z_range(before, 0, 1)
            products(n, rows_n, rows_n, per, after_own)
            for d in range(rows_n // per + 1, rows_n):
                send_z_range(before, d, 1)
            send_z_range(order[place - 2], rows_n - 1, 1)
            for d in range(rows_n):
                send_z_range(n, d, 1)
    for n in order[-4:-1]:
        finish(n)
    for n in order[-4:-1]:
        drain(n)
    first = sum_narrow[0]
    second = finish(wides + 1)
    keep = low_lanes(owned // 2)
    out_ref[0, 0, : owned // 2, last] = jnp.where(keep, first, swap(second)).astype(bf16)
    out_ref[0, 0, owned // 2 :, last] = jnp.where(keep, swap(first), second).astype(bf16)

    masks.wait_send()
    drain(chunks - 1)


def fused(inverse, factor, block_mask, pole_real, pole_imaginary):
    rows_n = lax.axis_size("row")
    height, width = inverse.shape[2:]
    depth, columns_all = factor.shape[2:]
    wides = columns_all // LANES - 1
    chunks = wides + 2
    owned = height // (rows_n * 4)
    half = owned // 2
    steps = 2 * rows_n
    f32, bf16, i16 = jnp.float32, jnp.bfloat16, jnp.int16
    dma = pltpu.SemaphoreType.DMA
    big = pl.BlockSpec(memory_space=pltpu.HBM)

    def both(lead, rows, kind):
        return [
            pltpu.VMEM((wides,) + lead + (rows[0], LANES), kind),
            pltpu.VMEM((2,) + lead + (rows[1], LANES), kind),
        ]

    full = (owned, half)
    coded = (owned + 16, half + 16)
    return pl.pallas_call(
        functools.partial(kernel, rows_n),
        out_shape=jax.ShapeDtypeStruct((1, 1, owned, columns_all), jnp.bfloat16),
        in_specs=[big] * 5,
        out_specs=pl.BlockSpec(memory_space=pltpu.VMEM),
        scratch_shapes=[
            pltpu.VMEM((height, 2 * depth), bf16),
            pltpu.VMEM((height, 2 * depth), bf16),
            pltpu.VMEM((2, depth, columns_all), bf16),
            pltpu.VMEM((wides, 2, depth, LANES), bf16),
            pltpu.VMEM((2, depth, LANES), bf16),
            pltpu.VMEM((2, depth, LANES), bf16),
            pltpu.SMEM(pole_real.shape, f32),
            pltpu.SMEM(pole_imaginary.shape, f32),
            pltpu.VMEM(block_mask.shape, block_mask.dtype),
            pltpu.VMEM(block_mask.shape, block_mask.dtype),
            pltpu.VMEM((2, block_mask.shape[0], depth, LANES), f32),
            pltpu.VMEM((2 * depth, 2 * columns_all), bf16),
            pltpu.VMEM((2 * depth, 2 * LANES), bf16),
            pltpu.VMEM((2 * depth, LANES), bf16),
            *both((steps, 2), full, f32),
            *both((steps,), full, f32),
            *both((rows_n,), coded, i16),
            *both((rows_n,), coded, i16),
            *both((rows_n - 1,), coded, i16),
            *both((rows_n - 1,), coded, i16),
            *both((), full, f32),
            dma((2, 2, steps)),
            dma((wides + 1,)),
            dma((3,)),
            dma((chunks,)),
            dma((chunks,)),
            dma,
            dma,
            dma((chunks,)),
            dma((chunks, steps)),
            dma((chunks,)),
            dma((chunks, rows_n)),
            dma((chunks,)),
            dma((chunks, rows_n)),
        ],
        compiler_params=pltpu.CompilerParams(
            collective_id=0, has_side_effects=True, vmem_limit_bytes=53 * 1024 * 1024
        ),
    )(pole_real, pole_imaginary, block_mask, factor, inverse)


def solution(mesh):
    sizes = dict(mesh.shape)

    def shards(inverse, factor, block_mask, pole_real, pole_imaginary):
        supers = block_mask.shape[0]
        wide = factor.shape[3] // supers
        small = 2 * inverse.shape[2] * inverse.shape[3] * 2 <= 20 * 1024 * 1024
        fits = sizes["pole"] == 4 and sizes["col"] == 2 and sizes["row"] >= 2
        owned = inverse.shape[2] // (sizes["row"] * 4)
        if fits and small and wide % LANES == 0 and owned % 32 == 0:
            body = fused
        else:
            body = plain
        return body(inverse, factor, block_mask, pole_real, pole_imaginary)

    return jax.shard_map(
        shards,
        mesh=mesh,
        in_specs=(
            P("pole", None, "col", "row"),
            P("pole", None, ("row", "col"), None),
            P(None, ("row", "col")),
            P("pole"),
            P("pole"),
        ),
        out_specs=P("col", "row", "pole", None),
        check_vma=False,
    )
```
